32 devices in a mesh: row: 8 (over z, core), col: 4 (over y, x).
Axes of the slice: x: 2, y: 2, z: 4, core: 2. Of those that a mesh axis runs over, the one named last changes fastest.
Arguments:
- inputs: bfloat16 [1024, 12288], P('col', 'row'), may hold values from -6 to 6
- segments: int32 [8, 1536], P('row'), may hold values from 0 to 3, never falling along the last dimension, each value on 1 to 768 neighbouring positions
- ln1_gain: bfloat16 [1024], P('col'), may hold values from 0.5 to 1.5
- ln1_bias: bfloat16 [1024], P('col'), may hold values from -1.75 to 1.75
- ln2_gain: bfloat16 [1024], P('col'), may hold values from 0.5 to 1.5
- ln2_bias: bfloat16 [1024], P('col'), may hold values from -1.75 to 1.75
- qkv_weight: bfloat16 [1024, 3072], P('row', 'col'), may hold values from -0.1875 to 0.1875
- qkv_bias: bfloat16 [3072], P('col'), may hold values from -1.75 to 1.75
- attn_weight: bfloat16 [1024, 1024], P('col', 'row'), may hold values from -0.75 to 0.75
- attn_bias: bfloat16 [1024], P('col'), may hold values from -1.75 to 1.75
- in_weight: bfloat16 [1024, 4096], P('row', 'col'), may hold values from -0.1875 to 0.1875
- in_bias: bfloat16 [4096], P('col'), may hold values from -1.75 to 1.75
- mlp_weight: bfloat16 [4096, 1024], P('col', 'row'), may hold values from -0.09375 to 0.09375
- mlp_bias: bfloat16 [1024], P('col'), may hold values from -1.75 to 1.75
- cotangent: bfloat16 [1024, 12288], P('col', 'row'), may hold values from -6 to 6
Outputs:
- output: bfloat16 [1024, 12288], P('col', 'row')
- grad_inputs: float32 [1024, 12288], P('col', 'row')
- grad_ln1_gain: float32 [1024], P('col')
- grad_ln1_bias: float32 [1024], P('col')
- grad_ln2_gain: float32 [1024], P('col')
- grad_ln2_bias: float32 [1024], P('col')
- grad_qkv_weight: float32 [1024, 3072], P('row', 'col')
- grad_qkv_bias: float32 [3072], P('col')
- grad_attn_weight: float32 [1024, 1024], P('col', 'row')
- grad_attn_bias: float32 [1024], P('col')
- grad_in_weight: float32 [1024, 4096], P('row', 'col')
- grad_in_bias: float32 [4096], P('col')
- grad_mlp_weight: float32 [4096, 1024], P('col', 'row')
- grad_mlp_bias: float32 [1024], P('col')
The draws below stay inside these ranges and needn't reach their ends.
Inputs may be any that keep to these rules, and one draw needn't show every extreme that they name: `segments`: along each sequence the document numbers never fall; each of the 4 documents holds 1 to 768 tokens, and in each sequence one holds exactly 768.
All inputs are finite; a program needn't handle non-finite values.
Results may differ from the reference program's by a relative error of at most 0.014.
Values may be sent and summed in bfloat16 or wider, within the bound.
No kernel may reach another device: no remote copies, remote signals or barrier semaphores. Data moves between devices by JAX's collectives and lax.ppermute only.
A program may use at most 128 MiB of HBM per device.

```python
import math
import jax
import jax.numpy as jnp
import numpy as np
from jax import lax

D = 1024
H = 16
HEAD = 64
ROT = 16
FF = 4096
SEQ = 1536
DOCS = 4
SEQS = 8
TOKENS = 12288


def block_scale(rng, dims, cuts, smallest, largest):
    def one(dim, shards_of):
        steps = jax.random.uniform(jax.random.fold_in(jax.random.fold_in(rng, 6), dim), (shards_of,), jnp.float32, smallest / len(cuts), largest / len(cuts))
        return jnp.repeat(jnp.exp(steps), dims[dim] // shards_of).reshape((-1,) + (1,) * (len(dims) - dim - 1))

    factor_of = one(*cuts[0])
    for cut in cuts[1:]:
        factor_of = factor_of * one(*cut)
    return factor_of


def split_up(amount, total, limit, lean):
    loads = [(1 << 20) // math.isqrt(grade ** lean) + 1 for grade in range(2, amount + 1)]
    spare, given = total - limit - (amount - 1), [1] * (amount - 1)
    while spare > 0:
        movable = [i for i in range(amount - 1) if given[i] < limit]
        mass, left = sum([loads[i] for i in movable]), spare
        for i in movable:
            more = min(limit - given[i], max(1, left * loads[i] // mass), spare)
            given[i] = given[i] + more
            spare = spare - more
    return np.array([limit] + given)


def ragged(key, number_of, total, bound, slope):
    if number_of == 2:
        one = jax.random.randint(key, (), max(1, total - bound), min(bound, total - 1) + 1)
        return jnp.stack([one, total - one])
    sizes = jnp.asarray(split_up(number_of, total, bound, slope), jnp.int32)
    twos = (number_of - 1) // 2
    giver, receiver = sizes[1:1 + 2 * twos:2], sizes[2:2 + 2 * twos:2]
    margin = jnp.minimum(giver - 1, bound - receiver)
    passed = jax.random.randint(jax.random.fold_in(key, 1), (twos,), 0, 1 << 20) % (margin + 1)
    sizes = sizes.at[1:1 + 2 * twos:2].set(giver - passed).at[2:2 + 2 * twos:2].set(receiver + passed)
    return sizes[jax.random.permutation(jax.random.fold_in(key, 2), number_of)]


def bell_draw(stream_key, shape, deviation, bound, split=(), held_as=jnp.bfloat16):
    array = jax.random.normal(stream_key, shape, jnp.float32) * deviation
    if len(split) > 0:
        array = block_scale(stream_key, shape, split, -0.22, 0.18) * array
    return jnp.clip(array, min=-bound, max=bound).astype(held_as)


def setup_inputs(seed: int = 0) -> dict:
    key_list = jax.random.split(jax.random.key(seed), 16)
    return {
        "inputs": bell_draw(key_list[0], (D, TOKENS), 1.0, 6.0, ((0, 4), (1, 8))),
        "segments": jax.vmap(lambda own: jnp.searchsorted(jnp.cumsum(ragged(own, DOCS, SEQ, SEQ // 2, 1)), jnp.arange(SEQ), side="right"))(jax.random.split(key_list[1], SEQS)).reshape((SEQS, SEQ)).astype(jnp.int32),
        "ln1_gain": jnp.clip(1.0 + 0.1 * jax.random.normal(key_list[2], (D,), jnp.float32), 0.5, 1.5).astype(jnp.bfloat16),
        "ln1_bias": bell_draw(key_list[3], (D,), 0.3, 1.75, ((0, 4),)),
        "ln2_gain": jnp.clip(1.0 + 0.1 * jax.random.normal(key_list[4], (D,), jnp.float32), 0.5, 1.5).astype(jnp.bfloat16),
        "ln2_bias": bell_draw(key_list[5], (D,), 0.3, 1.75, ((0, 4),)),
        "qkv_weight": bell_draw(key_list[6], (D, 3 * D), D ** -0.5, 0.1875, ((0, 8), (1, 4))),
        "qkv_bias": bell_draw(key_list[7], (3 * D,), 0.3, 1.75, ((0, 4),)),
        "attn_weight": bell_draw(key_list[8], (D, D), (D // 16) ** -0.5, 0.75, ((0, 4), (1, 8))),
        "attn_bias": bell_draw(key_list[9], (D,), 0.3, 1.75, ((0, 4),)),
        "in_weight": bell_draw(key_list[10], (D, FF), D ** -0.5, 0.1875, ((0, 8), (1, 4))),
        "in_bias": bell_draw(key_list[11], (FF,), 0.3, 1.75, ((0, 4),)),
        "mlp_weight": bell_draw(key_list[12], (FF, D), FF ** -0.5, 0.09375, ((0, 4), (1, 8))),
        "mlp_bias": bell_draw(key_list[13], (D,), 0.3, 1.75, ((0, 4),)),
        "cotangent": bell_draw(key_list[14], (D, TOKENS), 1.0, 6.0, ((0, 4), (1, 8))),
    }


EPSILON = 1e-05
MASK_FILL = -1e+30
PRECISE = lax.Precision.HIGHEST

@jax.custom_vjp
def low(v):
    return lax.optimization_barrier(v.astype(jnp.bfloat16)).astype(jnp.float32)

@jax.custom_vjp
def low_back(v):
    return v

def low_keep(v):
    return (low(v), None)

def low_pass(kept, grad):
    return (grad,)

def back_keep(v):
    return (v, None)

def back_low(kept, grad):
    return (low(grad),)
low.defvjp(low_keep, low_pass)
low_back.defvjp(back_keep, back_low)

def doc_starts(segment_row):
    places = jnp.arange(segment_row.shape[0], dtype=jnp.int32)
    earlier = jnp.concatenate([segment_row[:1] - 1, segment_row[:-1]])
    change_marks = jnp.where(segment_row != earlier, places, jnp.zeros_like(places))
    return lax.cummax(change_marks, axis=0)

def rotary_tables(starts, rotary):
    places = jnp.arange(starts.shape[0], dtype=jnp.int32)
    offset = (places - starts).astype(jnp.float32)
    halfway = rotary // 2
    frequency = 10000.0 ** (-2.0 * jnp.arange(halfway, dtype=jnp.float32) / rotary)
    angles = offset[:, None] * frequency[None, :]
    cosine = jnp.concatenate([jnp.cos(angles), jnp.cos(angles)], 1)
    sine_table = jnp.concatenate([jnp.sin(angles), jnp.sin(angles)], 1)
    return (cosine, sine_table)

def rotate(values, cosine, sine_table):
    rotary = cosine.shape[1]
    halfway = rotary // 2
    turned = values[..., :rotary]
    swapped = jnp.concatenate([-turned[..., halfway:], turned[..., :halfway]], -1)
    return jnp.concatenate([turned * cosine + swapped * sine_table, values[..., rotary:]], -1)

def attention(query_heads, key_heads, value_heads, starts):
    length = query_heads.shape[1]
    block_rows = min(512, length)
    block_count = length // block_rows
    score_scale = HEAD ** (-0.5)
    places = jnp.arange(length, dtype=jnp.int32)

    def one_block(pieces):
        query_block, block_start = pieces
        row_index = block_start + jnp.arange(block_rows, dtype=jnp.int32)
        row_starts = lax.dynamic_slice_in_dim(starts, block_start, block_rows)
        allowed = (places[None, :] <= row_index[:, None]) & (places[None, :] >= row_starts[:, None])
        raw_scores = low_back(jnp.einsum('hqe,hke->hqk', query_block, key_heads, precision=PRECISE) * score_scale)
        scores = jnp.where(allowed[None], raw_scores, MASK_FILL)
        weights = jax.nn.softmax(scores, axis=-1)
        return low_back(jnp.einsum('hqk,hke->hqe', low(weights), value_heads, precision=PRECISE))
    query_blocks = query_heads.reshape(query_heads.shape[0], block_count, block_rows, query_heads.shape[2]).transpose(1, 0, 2, 3)
    block_starts = jnp.arange(block_count, dtype=jnp.int32) * block_rows
    results = lax.map(jax.checkpoint(one_block), (query_blocks, block_starts))
    return results.transpose(1, 0, 2, 3).reshape(query_heads.shape)

def forward_layer(inputs, params, cosine, sine_table, starts):
    ln1_gain, ln1_bias, ln2_gain, ln2_bias, qkv_weight, qkv_bias, attn_weight, attn_bias, in_weight, in_bias, mlp_weight, mlp_bias = params
    average = lax.optimization_barrier(jnp.mean(inputs, axis=1, keepdims=True))
    centred = inputs - average
    spread = lax.optimization_barrier(jnp.mean(centred * centred, axis=1, keepdims=True))
    normed = centred * lax.rsqrt(spread + EPSILON)
    attn_in = low(normed * ln1_gain + ln1_bias)
    mlp_in = low(normed * ln2_gain + ln2_bias)
    joined_cols = low_back(jnp.dot(attn_in, qkv_weight, precision=PRECISE) + qkv_bias)
    joined_cols = joined_cols.reshape(SEQ, H, 3, HEAD).transpose(2, 1, 0, 3)
    query_heads = low(rotate(joined_cols[0], cosine, sine_table))
    key_heads = low(rotate(joined_cols[1], cosine, sine_table))
    value_heads = low(joined_cols[2])
    attended = attention(query_heads, key_heads, value_heads, starts)
    merged = low(attended.transpose(1, 0, 2).reshape(SEQ, D))
    hidden = low_back(jnp.dot(mlp_in, in_weight, precision=PRECISE) + in_bias)
    active = low(jax.nn.gelu(hidden, approximate=False))
    attn_out = jnp.dot(merged, attn_weight, precision=PRECISE) + attn_bias
    mlp_out = jnp.dot(active, mlp_weight, precision=PRECISE) + mlp_bias
    return inputs + attn_out + mlp_out

def reference(inputs, segments, ln1_gain, ln1_bias, ln2_gain, ln2_bias, qkv_weight, qkv_bias, attn_weight, attn_bias, in_weight, in_bias, mlp_weight, mlp_bias, cotangent):
    params = tuple((weight_item.astype(jnp.float32) for weight_item in (ln1_gain, ln1_bias, ln2_gain, ln2_bias, qkv_weight, qkv_bias, attn_weight, attn_bias, in_weight, in_bias, mlp_weight, mlp_bias)))
    sequences = inputs.astype(jnp.float32).T.reshape(SEQS, SEQ, D)
    cotangents = cotangent.astype(jnp.float32).T.reshape(SEQS, SEQ, D)

    def one_sequence(totals, pieces):
        layer_in, layer_cot, segment_row = pieces
        starts = doc_starts(segment_row)
        cosine, sine_table = rotary_tables(starts, ROT)

        def layer_apply(values, weights):
            return forward_layer(values, weights, cosine, sine_table, starts)
        output, pullback = jax.vjp(layer_apply, layer_in, params)
        grad_in, grad_params = pullback(layer_cot)
        totals = tuple((total + grad for total, grad in zip(totals, grad_params)))
        return (totals, (output.astype(jnp.bfloat16), grad_in))
    zero_grads = tuple((jnp.zeros(weight_item.shape, jnp.float32) for weight_item in params))
    totals, (outputs, grad_inputs) = lax.scan(one_sequence, zero_grads, (sequences, cotangents, segments))
    return (outputs.reshape(TOKENS, D).T, grad_inputs.reshape(TOKENS, D).T, totals[0], totals[1], totals[2], totals[3], totals[4], totals[5], totals[6], totals[7], totals[8], totals[9], totals[10], totals[11])
```

```python
import jax
import jax.numpy as jnp
from jax import lax
from jax.experimental import pallas as pl
from jax.experimental.pallas import tpu as pltpu
from jax.sharding import PartitionSpec as P

HEAD = 64
ROT = 16
HALF = ROT // 2
EPSILON = 1e-05
MASK_FILL = -1e30
BLOCK = 256
LONGEST = 768

F32 = jnp.float32
BF16 = jnp.bfloat16


def doc_starts(segment_row):
    places = jnp.arange(segment_row.shape[0], dtype=jnp.int32)
    earlier = jnp.concatenate([segment_row[:1] - 1, segment_row[:-1]])
    change_marks = jnp.where(segment_row != earlier, places, jnp.zeros_like(places))
    return lax.cummax(change_marks, axis=0)


def rotary_tables(starts):
    places = jnp.arange(starts.shape[0], dtype=jnp.int32)
    offset = (places - starts).astype(F32)
    frequency = 10000.0 ** (-2.0 * jnp.arange(HALF, dtype=F32) / ROT)
    angles = frequency[:, None] * offset[None, :]
    return jnp.cos(angles), jnp.sin(angles)


def gelu_pair(hidden):
    size = jnp.abs(hidden)
    t = 1.0 / (1.0 + (0.3275911 * 0.7071067811865476) * size)
    bell = jnp.exp(-0.5 * hidden * hidden)
    poly = t * (
        0.254829592
        + t * (-0.284496736 + t * (1.421413741 + t * (-1.453152027 + t * 1.061405429)))
    )
    tail = 0.5 * poly * bell
    phi = jnp.where(hidden >= 0.0, 1.0 - tail, tail)
    active = hidden * phi
    slope = phi + hidden * bell * 0.3989422804014327
    return active, slope


def dot(a, b, dims):
    return lax.dot_general(a, b, (dims, ((), ())), preferred_element_type=F32)


def attention_kernel(f_ref, do_ref, cos_ref, sin_ref, starts_ref, o_ref, df_ref, dk_ref, dv_ref):
    length = f_ref.shape[1]
    cos = cos_ref[...]
    sin = sin_ref[...]

    def rotated(base):
        low = f_ref[base : base + HALF, :]
        high = f_ref[base + HALF : base + ROT, :]
        rest = f_ref[base + ROT : base + HEAD, :]
        return jnp.concatenate([low * cos - high * sin, high * cos + low * sin, rest], 0)

    q = (rotated(0) * (HEAD**-0.5)).astype(BF16)
    k32 = rotated(HEAD)
    v32 = f_ref[2 * HEAD : 3 * HEAD, :]
    k = k32.astype(BF16)
    v = v32.astype(BF16)
    k_t = k32.T.astype(BF16)
    v_t = v32.T.astype(BF16)
    dk_ref[...] = jnp.zeros_like(dk_ref)
    dv_ref[...] = jnp.zeros_like(dv_ref)

    def put_rotated(base, at, grad):
        low = grad[:HALF]
        high = grad[HALF:ROT]
        c = cos[:, at]
        s = sin[:, at]
        df_ref[base : base + HEAD, at] = jnp.concatenate(
            [low * c + high * s, high * c - low * s, grad[ROT:]], 0
        ).astype(BF16)

    for first in range(0, length, BLOCK):
        here = slice(first, first + BLOCK)
        back = max(0, first - LONGEST)
        keys = slice(back, first + BLOCK)
        count = first + BLOCK - back
        scores = dot(k_t[keys], q[:, here], ((1,), (0,)))
        key_at = lax.broadcasted_iota(jnp.int32, (count, BLOCK), 0) + back
        query_at = lax.broadcasted_iota(jnp.int32, (count, BLOCK), 1) + first
        allowed = (key_at >= starts_ref[:, here]) & (key_at <= query_at)
        scores = jnp.where(allowed, scores, MASK_FILL)
        peak = jnp.max(scores, axis=0, keepdims=True)
        weight = jnp.exp(scores - peak)
        weight = weight * (1.0 / jnp.sum(weight, axis=0, keepdims=True))
        rounded = weight.astype(BF16)
        d_here = do_ref[:, here]
        o_ref[:, here] = dot(v[:, keys], rounded, ((1,), (0,))).astype(BF16)
        grad_w = dot(v_t[keys], d_here, ((1,), (0,)))
        delta = jnp.sum(weight * grad_w, axis=0, keepdims=True)
        grad_s = (weight * (grad_w - delta)).astype(BF16)
        put_rotated(0, here, dot(k[:, keys], grad_s, ((1,), (0,))) * (HEAD**-0.5))
        dk_ref[:, keys] += dot(q[:, here], grad_s, ((1,), (1,)))
        dv_ref[:, keys] += dot(d_here, rounded, ((1,), (1,)))
    put_rotated(HEAD, slice(0, length), dk_ref[...])
    df_ref[2 * HEAD : 3 * HEAD, :] = dv_ref[...].astype(BF16)


def attention(f, grad_o, cos, sin, starts):
    channels, length = f.shape
    heads = channels // (3 * HEAD)
    whole = lambda rows: pl.BlockSpec((rows, length), lambda h: (0, 0))
    per_head = lambda rows: pl.BlockSpec((rows, length), lambda h: (h, 0))
    return pl.pallas_call(
        attention_kernel,
        grid=(heads,),
        in_specs=[per_head(3 * HEAD), per_head(HEAD), whole(HALF), whole(HALF), whole(1)],
        out_specs=[per_head(HEAD), per_head(3 * HEAD)],
        out_shape=[
            jax.ShapeDtypeStruct((heads * HEAD, length), BF16),
            jax.ShapeDtypeStruct((channels, length), BF16),
        ],
        scratch_shapes=[pltpu.VMEM((HEAD, length), F32), pltpu.VMEM((HEAD, length), F32)],
        name="attention",
    )(f, grad_o, cos, sin, starts[None, :])


def xor_move(value, name, step):
    size = lax.axis_size(name)
    return lax.ppermute(value, name, [(i, i ^ step) for i in range(size)])


def z_move(value, step):
    size = lax.axis_size("row")
    return lax.ppermute(value, "row", [(i, (i + 2 * step) % size) for i in range(size)])


def col_gather(value):
    ncol = lax.axis_size("col")
    me = lax.axis_index("col")
    rows = value.shape[0]
    full = jnp.zeros((ncol * rows,) + value.shape[1:], value.dtype)
    for step in range(ncol):
        piece = xor_move(value, "col", step) if step else value
        full = lax.dynamic_update_slice_in_dim(full, piece, (me ^ step) * rows, 0)
    return full


def row_gather(value):
    nrow = lax.axis_size("row")
    nz = nrow // 2
    me = lax.axis_index("row")
    z, core = me // 2, me % 2
    rows = value.shape[0]
    full = jnp.zeros((nrow * rows,) + value.shape[1:], value.dtype)
    for step in range(nz):
        piece = z_move(value, step) if step else value
        source = (z - step + nz) % nz
        full = lax.dynamic_update_slice_in_dim(full, piece, (2 * source + core) * rows, 0)
        other = xor_move(piece, "row", 1)
        full = lax.dynamic_update_slice_in_dim(full, other, (2 * source + 1 - core) * rows, 0)
    return full


def col_scatter(value):
    ncol = lax.axis_size("col")
    me = lax.axis_index("col")
    rows = value.shape[0] // ncol
    part = lambda at: lax.dynamic_slice_in_dim(value, at * rows, rows, 0)
    total = part(me).astype(F32)
    for step in range(1, ncol):
        total = total + xor_move(part(me ^ step), "col", step).astype(F32)
    return total


def row_scatter(value):
    nrow = lax.axis_size("row")
    nz = nrow // 2
    me = lax.axis_index("row")
    z, core = me // 2, me % 2
    rows = value.shape[0] // nrow
    split = value.reshape((nz, 2, rows) + value.shape[1:])
    mine = lax.dynamic_index_in_dim(split, core, 1, False)
    other = lax.dynamic_index_in_dim(split, 1 - core, 1, False)
    chip = (mine.astype(F32) + xor_move(other, "row", 1).astype(F32)).astype(BF16)
    total = lax.dynamic_index_in_dim(chip, z, 0, False).astype(F32)
    for step in range(1, nz):
        piece = lax.dynamic_index_in_dim(chip, (z + step) % nz, 0, False)
        total = total + z_move(piece, step).astype(F32)
    return total


def row_sum(value):
    nrow = lax.axis_size("row")
    total = value
    for step in range(1, nrow):
        total = total + xor_move(value, "row", step)
    return total


def col_sum(value):
    total = value
    for step in range(1, lax.axis_size("col")):
        total = total + xor_move(value, "col", step)
    return total


def body(
    inputs,
    segments,
    ln1_gain,
    ln1_bias,
    ln2_gain,
    ln2_bias,
    qkv_weight,
    qkv_bias,
    attn_weight,
    attn_bias,
    in_weight,
    in_bias,
    mlp_weight,
    mlp_bias,
    cotangent,
):
    local_width, length = inputs.shape
    ncol = lax.axis_size("col")
    full_width = local_width * ncol
    me = lax.axis_index("col")
    column = lambda v: v.astype(F32)[:, None]
    starts = doc_starts(segments[0])
    cos, sin = rotary_tables(starts)

    x = col_gather(inputs)
    affine = col_gather(jnp.stack([ln1_gain, ln1_bias, ln2_gain, ln2_bias], 1)).astype(F32)
    w_qkv = row_gather(qkv_weight)
    w_attn = row_gather(attn_weight.T)
    w_in = row_gather(in_weight)
    w_mlp = row_gather(mlp_weight.T)
    dy = col_gather(cotangent)

    x32 = x.astype(F32)
    mean = jnp.sum(x32, axis=0, keepdims=True) / full_width
    centred = x32 - mean
    inverse = lax.rsqrt(jnp.sum(centred * centred, axis=0, keepdims=True) / full_width + EPSILON)
    normed = centred * inverse
    a1 = (normed * affine[:, 0:1] + affine[:, 1:2]).astype(BF16)
    a2 = (normed * affine[:, 2:3] + affine[:, 3:4]).astype(BF16)

    f = dot(w_qkv, a1, ((0,), (0,))) + column(qkv_bias)
    hidden = dot(w_in, a2, ((0,), (0,))) + column(in_bias)
    active, slope = gelu_pair(hidden)
    z = active.astype(BF16)
    slope = slope.astype(BF16)
    grad_o = dot(w_attn, dy, ((0,), (0,))).astype(BF16)
    grad_hidden = (dot(w_mlp, dy, ((0,), (0,))) * slope.astype(F32)).astype(BF16)

    mlp_grads = row_scatter(
        jnp.concatenate(
            [
                dot(a2, grad_hidden, ((1,), (1,))).astype(BF16),
                dot(dy, z, ((1,), (1,))).astype(BF16),
            ],
            1,
        )
    )

    o, df = attention(f, grad_o, cos, sin, starts)

    partial_out = (
        dot(w_attn, o, ((1,), (0,))) + dot(w_mlp, z, ((1,), (0,)))
    ).astype(BF16)
    summed_out = col_scatter(partial_out)
    local_in = inputs.astype(F32)
    output = (local_in + summed_out + column(attn_bias) + column(mlp_bias)).astype(BF16)

    attn_grads = row_scatter(
        jnp.concatenate(
            [
                dot(a1, df, ((1,), (1,))).astype(BF16),
                dot(dy, o, ((1,), (1,))).astype(BF16),
            ],
            1,
        )
    )

    back1 = dot(w_qkv, df, ((1,), (0,)))
    back2 = dot(w_in, grad_hidden, ((1,), (0,)))
    grad_n = back1 * affine[:, 0:1] + back2 * affine[:, 2:3]
    token_sums = col_sum(
        jnp.stack([jnp.sum(grad_n, axis=0), jnp.sum(grad_n * normed, axis=0)])
    )
    norm_parts = jnp.stack(
        [
            jnp.sum(back1 * normed, axis=1),
            jnp.sum(back1, axis=1),
            jnp.sum(back2 * normed, axis=1),
            jnp.sum(back2, axis=1),
        ]
    )
    grad_n_local = col_scatter(grad_n.astype(BF16))
    part = lambda at: lax.dynamic_slice_in_dim(norm_parts, at * local_width, local_width, 1)
    norm_sums = part(me)
    for step in range(1, ncol):
        norm_sums = norm_sums + xor_move(part(me ^ step), "col", step)

    vectors = [
        norm_sums.reshape(-1),
        jnp.sum(df, axis=1, dtype=F32),
        jnp.sum(cotangent, axis=1, dtype=F32),
        jnp.sum(grad_hidden, axis=1, dtype=F32),
    ]
    sizes = [v.shape[0] for v in vectors]
    sums = row_sum(jnp.concatenate(vectors))
    ends = [sum(sizes[: i + 1]) for i in range(len(sizes))]
    norm_out = sums[: ends[0]].reshape(4, local_width)
    grad_qkv_b = sums[ends[0] : ends[1]]
    grad_out_b = sums[ends[1] : ends[2]]
    grad_in_b = sums[ends[2] : ends[3]]

    normed_local = (local_in - mean) * inverse
    grad_input = cotangent.astype(F32) + inverse * (
        grad_n_local
        - token_sums[0:1] / full_width
        - normed_local * (token_sums[1:2] / full_width)
    )
    hidden_units = in_weight.shape[1]
    channels = qkv_weight.shape[1]
    return (
        output,
        grad_input,
        norm_out[0],
        norm_out[1],
        norm_out[2],
        norm_out[3],
        attn_grads[:, :channels],
        grad_qkv_b,
        attn_grads[:, channels:].T,
        grad_out_b,
        mlp_grads[:, :hidden_units],
        grad_in_b,
        mlp_grads[:, hidden_units:].T,
        grad_out_b,
    )


def solution(mesh):
    by_col = P("col")
    tokens = P("col", "row")
    into = P("row", "col")
    outof = P("col", "row")
    in_specs = (
        tokens,
        P("row", None),
        by_col,
        by_col,
        by_col,
        by_col,
        into,
        by_col,
        outof,
        by_col,
        into,
        by_col,
        outof,
        by_col,
        tokens,
    )
    out_specs = (
        tokens,
        tokens,
        by_col,
        by_col,
        by_col,
        by_col,
        into,
        by_col,
        outof,
        by_col,
        into,
        by_col,
        outof,
        by_col,
    )
    return jax.shard_map(body, mesh=mesh, in_specs=in_specs, out_specs=out_specs, check_vma=False)
```

```python
import jax
import jax.numpy as jnp
from jax import lax
from jax.experimental import pallas as pl
from jax.experimental.pallas import tpu as pltpu
from jax.sharding import PartitionSpec as P

HEAD = 64
ROT = 16
HALF = ROT // 2
EPSILON = 1e-05
MASK_FILL = -1e30
BLOCK = 256
LONGEST = 768

F32 = jnp.float32
BF16 = jnp.bfloat16


def doc_starts(segment_row):
    places = jnp.arange(segment_row.shape[0], dtype=jnp.int32)
    earlier = jnp.concatenate([segment_row[:1] - 1, segment_row[:-1]])
    change_marks = jnp.where(segment_row != earlier, places, jnp.zeros_like(places))
    return lax.cummax(change_marks, axis=0)


def rotary_tables(starts):
    places = jnp.arange(starts.shape[0], dtype=jnp.int32)
    offset = (places - starts).astype(F32)
    frequency = 10000.0 ** (-2.0 * jnp.arange(HALF, dtype=F32) / ROT)
    angles = frequency[:, None] * offset[None, :]
    return jnp.cos(angles), jnp.sin(angles)


def gelu_pair(hidden):
    size = jnp.abs(hidden)
    t = 1.0 / (1.0 + (0.3275911 * 0.7071067811865476) * size)
    bell = jnp.exp(-0.5 * hidden * hidden)
    poly = t * (
        0.254829592
        + t * (-0.284496736 + t * (1.421413741 + t * (-1.453152027 + t * 1.061405429)))
    )
    tail = 0.5 * poly * bell
    phi = jnp.where(hidden >= 0.0, 1.0 - tail, tail)
    active = hidden * phi
    slope = phi + hidden * bell * 0.3989422804014327
    return active, slope


def dot(a, b, dims):
    return lax.dot_general(a, b, (dims, ((), ())), preferred_element_type=F32)


def attention_kernel(f_ref, do_ref, cos_ref, sin_ref, starts_ref, o_ref, df_ref, dk_ref, dv_ref):
    length = f_ref.shape[1]
    cos = cos_ref[...]
    sin = sin_ref[...]

    def rotated(base):
        low = f_ref[base : base + HALF, :]
        high = f_ref[base + HALF : base + ROT, :]
        rest = f_ref[base + ROT : base + HEAD, :]
        return jnp.concatenate([low * cos - high * sin, high * cos + low * sin, rest], 0)

    q = (rotated(0) * (HEAD**-0.5)).astype(BF16)
    k32 = rotated(HEAD)
    v32 = f_ref[2 * HEAD : 3 * HEAD, :]
    k = k32.astype(BF16)
    v = v32.astype(BF16)
    k_t = k32.T.astype(BF16)
    v_t = v32.T.astype(BF16)
    dk_ref[...] = jnp.zeros_like(dk_ref)
    dv_ref[...] = jnp.zeros_like(dv_ref)

    def put_rotated(base, at, grad):
        low = grad[:HALF]
        high = grad[HALF:ROT]
        c = cos[:, at]
        s = sin[:, at]
        df_ref[base : base + HEAD, at] = jnp.concatenate(
            [low * c + high * s, high * c - low * s, grad[ROT:]], 0
        ).astype(BF16)

    for first in range(0, length, BLOCK):
        here = slice(first, first + BLOCK)
        back = max(0, first - LONGEST)
        keys = slice(back, first + BLOCK)
        count = first + BLOCK - back
        scores = dot(k_t[keys], q[:, here], ((1,), (0,)))
        key_at = lax.broadcasted_iota(jnp.int32, (count, BLOCK), 0) + back
        query_at = lax.broadcasted_iota(jnp.int32, (count, BLOCK), 1) + first
        allowed = (key_at >= starts_ref[:, here]) & (key_at <= query_at)
        scores = jnp.where(allowed, scores, MASK_FILL)
        peak = jnp.max(scores, axis=0, keepdims=True)
        weight = jnp.exp(scores - peak)
        weight = weight * (1.0 / jnp.sum(weight, axis=0, keepdims=True))
        rounded = weight.astype(BF16)
        d_here = do_ref[:, here]
        o_ref[:, here] = dot(v[:, keys], rounded, ((1,), (0,))).astype(BF16)
        grad_w = dot(v_t[keys], d_here, ((1,), (0,)))
        delta = jnp.sum(weight * grad_w, axis=0, keepdims=True)
        grad_s = (weight * (grad_w - delta)).astype(BF16)
        put_rotated(0, here, dot(k[:, keys], grad_s, ((1,), (0,))) * (HEAD**-0.5))
        dk_ref[:, keys] += dot(q[:, here], grad_s, ((1,), (1,)))
        dv_ref[:, keys] += dot(d_here, rounded, ((1,), (1,)))
    put_rotated(HEAD, slice(0, length), dk_ref[...])
    df_ref[2 * HEAD : 3 * HEAD, :] = dv_ref[...].astype(BF16)


def attention(f, grad_o, cos, sin, starts):
    channels, length = f.shape
    heads = channels // (3 * HEAD)
    whole = lambda rows: pl.BlockSpec((rows, length), lambda h: (0, 0))
    per_head = lambda rows: pl.BlockSpec((rows, length), lambda h: (h, 0))
    return pl.pallas_call(
        attention_kernel,
        grid=(heads,),
        in_specs=[per_head(3 * HEAD), per_head(HEAD), whole(HALF), whole(HALF), whole(1)],
        out_specs=[per_head(HEAD), per_head(3 * HEAD)],
        out_shape=[
            jax.ShapeDtypeStruct((heads * HEAD, length), BF16),
            jax.ShapeDtypeStruct((channels, length), BF16),
        ],
        scratch_shapes=[pltpu.VMEM((HEAD, length), F32), pltpu.VMEM((HEAD, length), F32)],
        cost_estimate=pl.CostEstimate(
            flops=24 * channels * length * LONGEST, transcendentals=0, bytes_accessed=0
        ),
        name="attention",
    )(f, grad_o, cos, sin, starts[None, :])


def xor_move(value, name, step):
    size = lax.axis_size(name)
    return lax.ppermute(value, name, [(i, i ^ step) for i in range(size)])


def log_sum(value, name):
    size = lax.axis_size(name)
    step = 1
    while step < size:
        value = value + xor_move(value, name, step)
        step *= 2
    return value


def col_pieces(value):
    return [value] + [xor_move(value, "col", s) for s in range(1, lax.axis_size("col"))]


def col_parts(value):
    ncol = lax.axis_size("col")
    me = lax.axis_index("col")
    rows = value.shape[0] // ncol
    return [lax.dynamic_slice_in_dim(value, (me ^ s) * rows, rows, 0) for s in range(ncol)]


def col_scatter(parts):
    total = parts[0].astype(F32)
    for step in range(1, len(parts)):
        total = total + xor_move(parts[step], "col", step).astype(F32)
    return total


def row_gather(value):
    return lax.all_gather(value, "row", axis=0, tiled=True)


def row_scatter(value):
    return lax.psum_scatter(value, "row", scatter_dimension=0, tiled=True).astype(F32)


def norm_kernel(at_ref, *refs):
    count = at_ref.shape[0]
    pieces = refs[:count]
    affine_ref, a1_ref, a2_ref, x_ref, stats_ref = refs[count:]
    rows, lanes = pieces[0].shape
    width = count * rows
    total = jnp.zeros((1, lanes), F32)
    for piece in pieces:
        total = total + jnp.sum(piece[...].astype(F32), axis=0, keepdims=True)
    mean = total / width
    spread = jnp.zeros((1, lanes), F32)
    for piece in pieces:
        centred = piece[...].astype(F32) - mean
        spread = spread + jnp.sum(centred * centred, axis=0, keepdims=True)
    inverse = lax.rsqrt(spread / width + EPSILON)
    for place, piece in enumerate(pieces):
        where = pl.ds(pl.multiple_of(at_ref[place] * rows, rows), rows)
        value = piece[...]
        normed = (value.astype(F32) - mean) * inverse
        affine = affine_ref[where, :]
        a1_ref[where, :] = (normed * affine[:, 0:1] + affine[:, 1:2]).astype(BF16)
        a2_ref[where, :] = (normed * affine[:, 2:3] + affine[:, 3:4]).astype(BF16)
        x_ref[where, :] = value
    stats_ref[0:1, :] = mean
    stats_ref[1:2, :] = inverse


def norm_inputs(pieces, affine, places):
    count = len(pieces)
    length = pieces[0].shape[1]
    width = affine.shape[0]
    rows = width // count
    wide = pl.BlockSpec((width, BLOCK), lambda j, at: (0, j))
    big = jax.ShapeDtypeStruct((width, length), BF16)
    return pl.pallas_call(
        norm_kernel,
        grid_spec=pltpu.PrefetchScalarGridSpec(
            num_scalar_prefetch=1,
            grid=(length // BLOCK,),
            in_specs=[pl.BlockSpec((rows, BLOCK), lambda j, at: (0, j))] * count
            + [pl.BlockSpec((width, 4), lambda j, at: (0, 0))],
            out_specs=[wide, wide, wide, pl.BlockSpec((2, BLOCK), lambda j, at: (0, j))],
        ),
        out_shape=[big, big, big, jax.ShapeDtypeStruct((2, length), F32)],
        name="norm",
    )(places, *pieces, affine)


def place_kernel(at_ref, *refs):
    out_ref = refs[-1]
    for place, piece in enumerate(refs[:-1]):
        rows = piece.shape[0]
        out_ref[pl.ds(pl.multiple_of(at_ref[place] * rows, rows), rows), :] = piece[...]


def place_pieces(pieces, places):
    count = len(pieces)
    rows, length = pieces[0].shape
    return pl.pallas_call(
        place_kernel,
        grid_spec=pltpu.PrefetchScalarGridSpec(
            num_scalar_prefetch=1,
            grid=(length // BLOCK,),
            in_specs=[pl.BlockSpec((rows, BLOCK), lambda j, at: (0, j))] * count,
            out_specs=pl.BlockSpec((count * rows, BLOCK), lambda j, at: (0, j)),
        ),
        out_shape=jax.ShapeDtypeStruct((count * rows, length), pieces[0].dtype),
        name="place",
    )(places, *pieces)


def body(
    inputs,
    segments,
    ln1_gain,
    ln1_bias,
    ln2_gain,
    ln2_bias,
    qkv_weight,
    qkv_bias,
    attn_weight,
    attn_bias,
    in_weight,
    in_bias,
    mlp_weight,
    mlp_bias,
    cotangent,
):
    local_width, length = inputs.shape
    ncol = lax.axis_size("col")
    full_width = local_width * ncol
    me = lax.axis_index("col")
    column = lambda v: v.astype(F32)[:, None]
    starts = doc_starts(segments[0])
    cos, sin = rotary_tables(starts)

    places = me ^ jnp.arange(ncol, dtype=jnp.int32)
    channels = qkv_weight.shape[1]
    hidden_units = in_weight.shape[1]
    side = jnp.concatenate([ln1_gain, ln1_bias, ln2_gain, ln2_bias])
    side = jnp.pad(side[None, :], ((0, 15), (0, length - side.shape[0])))
    pieces = col_pieces(jnp.concatenate([inputs, side], 0))
    w_first = row_gather(jnp.concatenate([qkv_weight, attn_weight.T], 1))
    w_second = row_gather(jnp.concatenate([in_weight, mlp_weight.T], 1))
    dy = place_pieces(col_pieces(cotangent), places)
    w_qkv, w_attn = w_first[:, :channels], w_first[:, channels:]
    w_in, w_mlp = w_second[:, :hidden_units], w_second[:, hidden_units:]

    affine = jnp.stack([p[local_width, : 4 * local_width].reshape(4, local_width) for p in pieces])
    affine = affine[places].transpose(0, 2, 1).reshape(full_width, 4).astype(F32)
    a1, a2, x, stats = norm_inputs(pieces, affine, places)
    mean, inverse = stats[0:1], stats[1:2]

    f = dot(w_qkv, a1, ((0,), (0,))) + column(qkv_bias)
    grad_o = dot(w_attn, dy, ((0,), (0,))).astype(BF16)
    o, df = attention(f, grad_o, cos, sin, starts)
    attn_raw = jnp.concatenate(
        [
            dot(a1, df, ((1,), (1,))).astype(BF16),
            dot(dy, o, ((1,), (1,))).astype(BF16),
        ],
        1,
    )
    attn_raw, a2 = lax.optimization_barrier((attn_raw, a2))
    attn_grads = row_scatter(attn_raw)

    hidden = dot(w_in, a2, ((0,), (0,))) + column(in_bias)
    active, slope = gelu_pair(hidden)
    z = active.astype(BF16)
    slope = slope.astype(BF16)
    mlp_raw = dot(dy, z, ((1,), (1,))).astype(BF16)
    partial_out = (dot(w_attn, o, ((1,), (0,))) + dot(w_mlp, z, ((1,), (0,)))).astype(BF16)
    out_parts = col_parts(partial_out)
    mlp_raw, out_parts, dy = lax.optimization_barrier((mlp_raw, out_parts, dy))
    mlp_grads = row_scatter(mlp_raw)
    summed_out = col_scatter(out_parts)
    local_in = inputs.astype(F32)
    output = (local_in + summed_out + column(attn_bias) + column(mlp_bias)).astype(BF16)

    grad_hidden = (dot(w_mlp, dy, ((0,), (0,))) * slope.astype(F32)).astype(BF16)
    in_raw = dot(a2, grad_hidden, ((1,), (1,))).astype(BF16)
    in_raw, grad_hidden = lax.optimization_barrier((in_raw, grad_hidden))
    in_grads = row_scatter(in_raw)

    normed = (x.astype(F32) - mean) * inverse
    back1 = dot(w_qkv, df, ((1,), (0,)))
    back2 = dot(w_in, grad_hidden, ((1,), (0,)))
    grad_n = back1 * affine[:, 0:1] + back2 * affine[:, 2:3]
    n_parts = col_parts(grad_n.astype(BF16))
    grad_n_local = col_scatter(n_parts)
    over_col = jnp.concatenate(
        [
            jnp.sum(grad_n, axis=0),
            jnp.sum(grad_n * normed, axis=0),
            jnp.sum(back1 * normed, axis=1),
            jnp.sum(back1, axis=1),
            jnp.sum(back2 * normed, axis=1),
            jnp.sum(back2, axis=1),
        ]
    )
    over_col = log_sum(over_col, "col")
    token_sums = over_col[: 2 * length].reshape(2, length)
    norm_sums = lax.dynamic_slice_in_dim(
        over_col[2 * length :].reshape(4, full_width), me * local_width, local_width, 1
    )

    vectors = [
        norm_sums.reshape(-1),
        jnp.sum(df, axis=1, dtype=F32),
        jnp.sum(cotangent, axis=1, dtype=F32),
        jnp.sum(grad_hidden, axis=1, dtype=F32),
    ]
    sizes = [v.shape[0] for v in vectors]
    sums = log_sum(jnp.concatenate(vectors), "row")
    ends = [sum(sizes[: i + 1]) for i in range(len(sizes))]
    norm_out = sums[: ends[0]].reshape(4, local_width)
    grad_qkv_b = sums[ends[0] : ends[1]]
    grad_out_b = sums[ends[1] : ends[2]]
    grad_in_b = sums[ends[2] : ends[3]]

    normed_local = (local_in - mean) * inverse
    grad_input = cotangent.astype(F32) + inverse * (
        grad_n_local
        - token_sums[0:1] / full_width
        - normed_local * (token_sums[1:2] / full_width)
    )
    return (
        output,
        grad_input,
        norm_out[0],
        norm_out[1],
        norm_out[2],
        norm_out[3],
        attn_grads[:, :channels],
        grad_qkv_b,
        attn_grads[:, channels:].T,
        grad_out_b,
        in_grads,
        grad_in_b,
        mlp_grads.T,
        grad_out_b,
    )


def solution(mesh):
    by_col = P("col")
    tokens = P("col", "row")
    into = P("row", "col")
    outof = P("col", "row")
    in_specs = (
        tokens,
        P("row", None),
        by_col,
        by_col,
        by_col,
        by_col,
        into,
        by_col,
        outof,
        by_col,
        into,
        by_col,
        outof,
        by_col,
        tokens,
    )
    out_specs = (
        tokens,
        tokens,
        by_col,
        by_col,
        by_col,
        by_col,
        into,
        by_col,
        outof,
        by_col,
        into,
        by_col,
        outof,
        by_col,
    )
    return jax.shard_map(body, mesh=mesh, in_specs=in_specs, out_specs=out_specs, check_vma=False)
```

```python
import jax
import jax.numpy as jnp
from jax import lax
from jax.experimental import pallas as pl
from jax.experimental.pallas import tpu as pltpu
from jax.sharding import PartitionSpec as P


HEAD = 64
ROT = 16
HALF = ROT // 2
EPSILON = 1e-05
MASK_FILL = -1e30
BLOCK = 256
LONGEST = 768
WIDE = 512

F32 = jnp.float32
BF16 = jnp.bfloat16


def doc_starts(segment_row):
    places = jnp.arange(segment_row.shape[0], dtype=jnp.int32)
    earlier = jnp.concatenate([segment_row[:1] - 1, segment_row[:-1]])
    change_marks = jnp.where(segment_row != earlier, places, jnp.zeros_like(places))
    return lax.cummax(change_marks, axis=0)


def rotary_tables(starts):
    places = jnp.arange(starts.shape[0], dtype=jnp.int32)
    offset = (places - starts).astype(F32)
    frequency = 10000.0 ** (-2.0 * jnp.arange(HALF, dtype=F32) / ROT)
    angles = frequency[:, None] * offset[None, :]
    return jnp.cos(angles), jnp.sin(angles)


def gelu_pair(hidden):
    size = jnp.abs(hidden)
    t = 1.0 / (1.0 + (0.3275911 * 0.7071067811865476) * size)
    bell = jnp.exp(-0.5 * hidden * hidden)
    poly = t * (
        0.254829592
        + t * (-0.284496736 + t * (1.421413741 + t * (-1.453152027 + t * 1.061405429)))
    )
    tail = 0.5 * poly * bell
    phi = jnp.where(hidden >= 0.0, 1.0 - tail, tail)
    active = hidden * phi
    slope = phi + hidden * bell * 0.3989422804014327
    return active, slope


def dot(a, b, dims):
    return lax.dot_general(a, b, (dims, ((), ())), preferred_element_type=F32)


def attention_kernel(f_ref, do_ref, cos_ref, sin_ref, starts_ref, o_ref, df_ref, dk_ref, dv_ref):
    length = f_ref.shape[1]
    cos = cos_ref[...]
    sin = sin_ref[...]

    def rotated(base):
        low = f_ref[base : base + HALF, :]
        high = f_ref[base + HALF : base + ROT, :]
        rest = f_ref[base + ROT : base + HEAD, :]
        return jnp.concatenate([low * cos - high * sin, high * cos + low * sin, rest], 0)

    q = (rotated(0) * (HEAD**-0.5)).astype(BF16)
    k32 = rotated(HEAD)
    v32 = f_ref[2 * HEAD : 3 * HEAD, :]
    k = k32.astype(BF16)
    v = v32.astype(BF16)
    k_t = k32.T.astype(BF16)
    v_t = v32.T.astype(BF16)
    dk_ref[...] = jnp.zeros_like(dk_ref)
    dv_ref[...] = jnp.zeros_like(dv_ref)

    def put_rotated(base, at, grad):
        low = grad[:HALF]
        high = grad[HALF:ROT]
        c = cos[:, at]
        s = sin[:, at]
        df_ref[base : base + HEAD, at] = jnp.concatenate(
            [low * c + high * s, high * c - low * s, grad[ROT:]], 0
        ).astype(BF16)

    for first in range(0, length, BLOCK):
        here = slice(first, first + BLOCK)
        back = max(0, first - LONGEST)
        keys = slice(back, first + BLOCK)
        count = first + BLOCK - back
        scores = dot(k_t[keys], q[:, here], ((1,), (0,)))
        key_at = lax.broadcasted_iota(jnp.int32, (count, BLOCK), 0) + back
        query_at = lax.broadcasted_iota(jnp.int32, (count, BLOCK), 1) + first
        allowed = (key_at >= starts_ref[:, here]) & (key_at <= query_at)
        scores = jnp.where(allowed, scores, MASK_FILL)
        peak = jnp.max(scores, axis=0, keepdims=True)
        weight = jnp.exp(scores - peak)
        weight = weight * (1.0 / jnp.sum(weight, axis=0, keepdims=True))
        rounded = weight.astype(BF16)
        d_here = do_ref[:, here]
        o_ref[:, here] = dot(v[:, keys], rounded, ((1,), (0,))).astype(BF16)
        grad_w = dot(v_t[keys], d_here, ((1,), (0,)))
        delta = jnp.sum(weight * grad_w, axis=0, keepdims=True)
        grad_s = (weight * (grad_w - delta)).astype(BF16)
        put_rotated(0, here, dot(k[:, keys], grad_s, ((1,), (0,))) * (HEAD**-0.5))
        dk_ref[:, keys] += dot(q[:, here], grad_s, ((1,), (1,)))
        dv_ref[:, keys] += dot(d_here, rounded, ((1,), (1,)))
    put_rotated(HEAD, slice(0, length), dk_ref[...])
    df_ref[2 * HEAD : 3 * HEAD, :] = dv_ref[...].astype(BF16)


def attention(f, grad_o, cos, sin, starts):
    channels, length = f.shape
    heads = channels // (3 * HEAD)
    whole = lambda rows: pl.BlockSpec((rows, length), lambda h: (0, 0))
    per_head = lambda rows: pl.BlockSpec((rows, length), lambda h: (h, 0))
    return pl.pallas_call(
        attention_kernel,
        grid=(heads,),
        in_specs=[per_head(3 * HEAD), per_head(HEAD), whole(HALF), whole(HALF), whole(1)],
        out_specs=[per_head(HEAD), per_head(3 * HEAD)],
        out_shape=[
            jax.ShapeDtypeStruct((heads * HEAD, length), BF16),
            jax.ShapeDtypeStruct((channels, length), BF16),
        ],
        scratch_shapes=[pltpu.VMEM((HEAD, length), F32), pltpu.VMEM((HEAD, length), F32)],
        cost_estimate=pl.CostEstimate(
            flops=24 * channels * length * LONGEST, transcendentals=0, bytes_accessed=0
        ),
        name="attention",
    )(f, grad_o, cos, sin, starts[None, :])


def xor_move(value, name, step):
    size = lax.axis_size(name)
    return lax.ppermute(value, name, [(i, i ^ step) for i in range(size)])


def log_sum(value, name):
    size = lax.axis_size(name)
    step = 1
    while step < size:
        value = value + xor_move(value, name, step)
        step *= 2
    return value


def col_pieces(value):
    return [value] + [xor_move(value, "col", s) for s in range(1, lax.axis_size("col"))]


def col_parts(value):
    ncol = lax.axis_size("col")
    me = lax.axis_index("col")
    rows = value.shape[0] // ncol
    return [lax.dynamic_slice_in_dim(value, (me ^ s) * rows, rows, 0) for s in range(ncol)]


def col_moves(parts):
    return parts[:1] + [xor_move(parts[step], "col", step) for step in range(1, len(parts))]


def add_parts(parts):
    total = parts[0].astype(F32)
    for part in parts[1:]:
        total = total + part.astype(F32)
    return total


def row_gather(value):
    return lax.all_gather(value, "row", axis=0, tiled=True)


def row_scatter(value):
    return lax.psum_scatter(value, "row", scatter_dimension=0, tiled=True).astype(F32)


def norm_kernel(at_ref, *refs):
    count = at_ref.shape[0]
    pieces = refs[:count]
    affine_ref, a1_ref, a2_ref, x_ref, stats_ref = refs[count:]
    rows, lanes = pieces[0].shape
    width = count * rows
    total = jnp.zeros((1, lanes), F32)
    for piece in pieces:
        total = total + jnp.sum(piece[...].astype(F32), axis=0, keepdims=True)
    mean = total / width
    spread = jnp.zeros((1, lanes), F32)
    for piece in pieces:
        centred = piece[...].astype(F32) - mean
        spread = spread + jnp.sum(centred * centred, axis=0, keepdims=True)
    inverse = lax.rsqrt(spread / width + EPSILON)
    for place, piece in enumerate(pieces):
        where = pl.ds(pl.multiple_of(at_ref[place] * rows, rows), rows)
        value = piece[...]
        normed = (value.astype(F32) - mean) * inverse
        affine = affine_ref[where, :]
        a1_ref[where, :] = (normed * affine[:, 0:1] + affine[:, 1:2]).astype(BF16)
        a2_ref[where, :] = (normed * affine[:, 2:3] + affine[:, 3:4]).astype(BF16)
        x_ref[where, :] = value
    stats_ref[0:1, :] = mean
    stats_ref[1:2, :] = inverse


def norm_inputs(pieces, affine, places):
    count = len(pieces)
    length = pieces[0].shape[1]
    width = affine.shape[0]
    rows = width // count
    wide = pl.BlockSpec((width, WIDE), lambda j, at: (0, j))
    big = jax.ShapeDtypeStruct((width, length), BF16)
    return pl.pallas_call(
        norm_kernel,
        grid_spec=pltpu.PrefetchScalarGridSpec(
            num_scalar_prefetch=1,
            grid=(length // WIDE,),
            in_specs=[pl.BlockSpec((rows, WIDE), lambda j, at: (0, j))] * count
            + [pl.BlockSpec((width, 4), lambda j, at: (0, 0))],
            out_specs=[wide, wide, wide, pl.BlockSpec((2, WIDE), lambda j, at: (0, j))],
        ),
        out_shape=[big, big, big, jax.ShapeDtypeStruct((2, length), F32)],
        name="norm",
    )(places, *pieces, affine)


def place_kernel(at_ref, *refs):
    out_ref = refs[-1]
    for place, piece in enumerate(refs[:-1]):
        rows = piece.shape[0]
        out_ref[pl.ds(pl.multiple_of(at_ref[place] * rows, rows), rows), :] = piece[...]


def place_pieces(pieces, places):
    count = len(pieces)
    rows, length = pieces[0].shape
    return pl.pallas_call(
        place_kernel,
        grid_spec=pltpu.PrefetchScalarGridSpec(
            num_scalar_prefetch=1,
            grid=(length // WIDE,),
            in_specs=[pl.BlockSpec((rows, WIDE), lambda j, at: (0, j))] * count,
            out_specs=pl.BlockSpec((count * rows, WIDE), lambda j, at: (0, j)),
        ),
        out_shape=jax.ShapeDtypeStruct((count * rows, length), pieces[0].dtype),
        name="place",
    )(places, *pieces)


def body(
    inputs,
    segments,
    ln1_gain,
    ln1_bias,
    ln2_gain,
    ln2_bias,
    qkv_weight,
    qkv_bias,
    attn_weight,
    attn_bias,
    in_weight,
    in_bias,
    mlp_weight,
    mlp_bias,
    cotangent,
):
    local_width, length = inputs.shape
    ncol = lax.axis_size("col")
    full_width = local_width * ncol
    me = lax.axis_index("col")
    column = lambda v: v.astype(F32)[:, None]
    starts = doc_starts(segments[0])
    cos, sin = rotary_tables(starts)

    places = me ^ jnp.arange(ncol, dtype=jnp.int32)
    channels = qkv_weight.shape[1]
    hidden_units = in_weight.shape[1]
    side = jnp.concatenate([ln1_gain, ln1_bias, ln2_gain, ln2_bias])
    side = jnp.pad(side[None, :], ((0, 15), (0, length - side.shape[0])))
    pieces = col_pieces(jnp.concatenate([inputs, side], 0))
    w_first = row_gather(jnp.concatenate([qkv_weight, attn_weight.T], 1))
    w_second = row_gather(jnp.concatenate([in_weight, mlp_weight.T], 1))
    cot_late = lax.optimization_barrier((cotangent, pieces[1:]))
    pieces = pieces[:1] + list(cot_late[1])
    dy = place_pieces(col_pieces(cot_late[0]), places)
    w_qkv, w_attn = w_first[:, :channels], w_first[:, channels:]
    w_in, w_mlp = w_second[:, :hidden_units], w_second[:, hidden_units:]

    affine = jnp.stack([p[local_width, : 4 * local_width].reshape(4, local_width) for p in pieces])
    affine = affine[places].transpose(0, 2, 1).reshape(full_width, 4).astype(F32)
    a1, a2, x, stats = norm_inputs(pieces, affine, places)
    mean, inverse = stats[0:1], stats[1:2]

    f = dot(w_qkv, a1, ((0,), (0,))) + column(qkv_bias)
    grad_o = dot(w_attn, dy, ((0,), (0,))).astype(BF16)
    o, df = attention(f, grad_o, cos, sin, starts)
    attn_raw = jnp.concatenate(
        [
            dot(a1, df, ((1,), (1,))).astype(BF16),
            dot(dy, o, ((1,), (1,))).astype(BF16),
        ],
        1,
    )
    attn_raw, a2 = lax.optimization_barrier((attn_raw, a2))
    attn_grads = row_scatter(attn_raw)

    hidden = dot(w_in, a2, ((0,), (0,))) + column(in_bias)
    active, slope = gelu_pair(hidden)
    z = active.astype(BF16)
    slope = slope.astype(BF16)
    mlp_raw = dot(dy, z, ((1,), (1,))).astype(BF16)
    partial_out = (dot(w_attn, o, ((1,), (0,))) + dot(w_mlp, z, ((1,), (0,)))).astype(BF16)
    out_parts = col_parts(partial_out)
    mlp_raw, out_parts, dy = lax.optimization_barrier((mlp_raw, out_parts, dy))
    mlp_grads = row_scatter(mlp_raw)
    out_moved = col_moves(out_parts)
    grad_hidden = (dot(w_mlp, dy, ((0,), (0,))) * slope.astype(F32)).astype(BF16)
    in_raw = dot(a2, grad_hidden, ((1,), (1,))).astype(BF16)
    in_raw, grad_hidden = lax.optimization_barrier((in_raw, grad_hidden))
    in_grads = row_scatter(in_raw)

    normed = (x.astype(F32) - mean) * inverse
    back1 = dot(w_qkv, df, ((1,), (0,)))
    back2 = dot(w_in, grad_hidden, ((1,), (0,)))
    grad_n = back1 * affine[:, 0:1] + back2 * affine[:, 2:3]
    over_col = jnp.concatenate(
        [
            jnp.sum(grad_n, axis=0),
            jnp.sum(grad_n * normed, axis=0),
            jnp.sum(back1 * normed, axis=1),
            jnp.sum(back1, axis=1),
            jnp.sum(back2 * normed, axis=1),
            jnp.sum(back2, axis=1),
        ]
    )
    over_col = log_sum(over_col, "col")
    n_parts, over_col, out_moved = lax.optimization_barrier(
        (col_parts(grad_n.astype(BF16)), over_col, out_moved)
    )
    grad_n_moved = col_moves(n_parts)
    local_in = inputs.astype(F32)
    output = (
        local_in + add_parts(out_moved) + column(attn_bias) + column(mlp_bias)
    ).astype(BF16)
    token_sums = over_col[: 2 * length].reshape(2, length)
    norm_sums = lax.dynamic_slice_in_dim(
        over_col[2 * length :].reshape(4, full_width), me * local_width, local_width, 1
    )

    vectors = [
        norm_sums.reshape(-1),
        jnp.sum(df, axis=1, dtype=F32),
        jnp.sum(cotangent, axis=1, dtype=F32),
        jnp.sum(grad_hidden, axis=1, dtype=F32),
    ]
    sizes = [v.shape[0] for v in vectors]
    sums = log_sum(jnp.concatenate(vectors), "row")
    sums, mean, inverse = lax.optimization_barrier((sums, mean, inverse))
    ends = [sum(sizes[: i + 1]) for i in range(len(sizes))]
    norm_out = sums[: ends[0]].reshape(4, local_width)
    grad_qkv_b = sums[ends[0] : ends[1]]
    grad_out_b = sums[ends[1] : ends[2]]
    grad_in_b = sums[ends[2] : ends[3]]

    grad_n_local = add_parts(grad_n_moved)
    normed_local = (local_in - mean) * inverse
    grad_input = cotangent.astype(F32) + inverse * (
        grad_n_local
        - token_sums[0:1] / full_width
        - normed_local * (token_sums[1:2] / full_width)
    )
    return (
        output,
        grad_input,
        norm_out[0],
        norm_out[1],
        norm_out[2],
        norm_out[3],
        attn_grads[:, :channels],
        grad_qkv_b,
        attn_grads[:, channels:].T,
        grad_out_b,
        in_grads,
        grad_in_b,
        mlp_grads.T,
        grad_out_b,
    )


def solution(mesh):
    by_col = P("col")
    tokens = P("col", "row")
    into = P("row", "col")
    outof = P("col", "row")
    in_specs = (
        tokens,
        P("row", None),
        by_col,
        by_col,
        by_col,
        by_col,
        into,
        by_col,
        outof,
        by_col,
        into,
        by_col,
        outof,
        by_col,
        tokens,
    )
    out_specs = (
        tokens,
        tokens,
        by_col,
        by_col,
        by_col,
        by_col,
        into,
        by_col,
        outof,
        by_col,
        into,
        by_col,
        outof,
        by_col,
    )

    return jax.shard_map(body, mesh=mesh, in_specs=in_specs, out_specs=out_specs, check_vma=False)
```
